512 devices in a mesh: dp: 128 (over z, y, core), mp: 4 (over x).
Axes of the slice: x: 4, y: 4, z: 16, core: 2. Of those that a mesh axis runs over, the one named last changes fastest.
Arguments:
- item_table: bfloat16 [262144, 256], P('dp'), may hold values from -6 to 6
- history_owner: int32 [32768, 1], P(('dp', 'mp')), may hold values from 0 to 127; in each aligned block of 64 rows (0 to 63, 64 to 127, ...) at most 4 rows name the same one
- history_row: int32 [32768], P(('dp', 'mp')), may hold values from 0 to 2047
- w_in: bfloat16 [256, 512], replicated, may hold values from -0.375 to 0.375
- conv_a: bfloat16 [4, 3, 512, 512], P(None, None, None, 'mp'), may hold values from -0.15625 to 0.15625
- conv_b: bfloat16 [4, 3, 512, 512], P(None, None, 'mp'), may hold values from -0.15625 to 0.15625
- gains: float32 [4, 512], replicated, may hold values from 0.5 to 1.5
- w_out: bfloat16 [512, 256], replicated, may hold values from -0.25 to 0.25
- cand_row: int32 [128, 128, 8], P('dp'), may hold values from 0 to 2047
- cand_count: int32 [128, 128], P('dp'), may hold values from 1 to 8, 512 in all within a row
- pos_owner: int32 [128], P('dp'), may hold values from 0 to 127
Outputs:
- scores: float32 [128, 128, 8], P('dp')
- user_loss: float32 [128], P('dp')
The draws below stay inside these ranges and needn't reach their ends.
Inputs may be any that keep to these rules, and one draw needn't show every extreme that they name: `history_owner`: within each aligned block of 64 events no owner appears more than 4 times, and some owner appears exactly 4 times. `cand_count`: each user's counts sum to 512; the largest of them is 8.
All inputs are finite; a program needn't handle non-finite values.
Results may differ from the reference program's by a relative error of at most 0.025.
Values may be sent and summed in bfloat16 or wider, within the bound.
No kernel may reach another device: no remote copies, remote signals or barrier semaphores. Data moves between devices by JAX's collectives and lax.ppermute only.
A program may use at most 64 MiB of HBM per device.

```python
import math
import jax
import jax.numpy as jnp
import numpy as np
from jax import lax

E = 256
C = 512
BLOCKS = 4
LEN = 256
ITEM_DEV = 2048
CPO = 8
USERS = 128
TOKENS = 32768
FETCH = 64
CAP = 4
ITEMS = 262144
NCAND = 512
N_DP = 128
N_MP = 4


def with_ends(values, key, smallest, largest):
    extent = values.shape
    index_at = [jax.random.randint(jax.random.fold_in(key, axis), (), 0, extent[axis]) for axis in range(len(extent))]
    values = values.at[tuple(index_at)].set(smallest)
    longest = extent.index(max(extent))
    index_at[longest] = (index_at[longest] + 1) % extent[longest]
    return values.at[tuple(index_at)].set(largest)


def steps_of(rng, extent, cuts, least, top_value):
    loudness, own = 1.0, jax.random.fold_in(rng, 6)
    for position, blocks in cuts:
        steps = jnp.exp(jax.random.uniform(jax.random.fold_in(own, position), (blocks,), jnp.float32, least / len(cuts), top_value / len(cuts)))
        loudness = loudness * jnp.repeat(steps, extent[position] // blocks).reshape([-1 if axis == position else 1 for axis in range(len(extent))])
    return loudness


def profile(amount, total, bound, skew):
    portions = [(1 << 20) // math.isqrt(grade ** skew) + 1 for grade in range(2, amount + 1)]
    rest, given = total - bound - (amount - 1), [1] * (amount - 1)
    while rest > 0:
        movable = [i for i in range(amount - 1) if given[i] < bound]
        pool, remaining = sum([portions[i] for i in movable]), rest
        for i in movable:
            addition = min(bound - given[i], max(1, remaining * portions[i] // pool), rest)
            given[i] = given[i] + addition
            rest = rest - addition
    return np.array([bound] + given)


def uneven_parts(own_key, amount, total, limit, skew):
    if amount == 2:
        one = jax.random.randint(own_key, (), max(1, total - limit), min(limit, total - 1) + 1)
        return jnp.stack([one, total - one])
    tallies = jnp.asarray(profile(amount, total, limit, skew), jnp.int32)
    couples = (amount - 1) // 2
    source_of, taker = tallies[1:1 + 2 * couples:2], tallies[2:2 + 2 * couples:2]
    slack = jnp.minimum(source_of - 1, limit - taker)
    passed = jax.random.randint(jax.random.fold_in(own_key, 1), (couples,), 0, 1 << 20) % (slack + 1)
    tallies = tallies.at[1:1 + 2 * couples:2].set(source_of - passed).at[2:2 + 2 * couples:2].set(taker + passed)
    return tallies[jax.random.permutation(jax.random.fold_in(own_key, 2), amount)]


def shared_out(rng, own, number, rows, count, top, limit, skew):
    sequence = jax.random.permutation(rng, count)
    crowded, usual = portions_of(count, rows * top, limit, skew, True), portions_of(count, rows * top, limit, skew, False)
    places = jnp.arange(count)

    def named(tallies, rotation):
        used = int((tallies > 0).sum())
        fixed = max(1, used // 4)
        passed = fixed + (places - fixed + rotation * (used - fixed)) % max(1, count - fixed)
        return jnp.zeros((count,), jnp.int32).at[sequence[jnp.where(places < fixed, places, passed)]].set(jnp.asarray(tallies, jnp.int32))

    tallies = jnp.where(number % 4 == 0, named(crowded, number // 4), named(usual, number - number // 4 - 1))
    mixed = jax.random.permutation(jax.random.fold_in(own, 3), count)
    giver, sink = mixed[0:count // 2 * 2:2], mixed[1:count // 2 * 2:2]
    margin = jnp.minimum(tallies[giver] - 1, limit - tallies[sink]) // 2
    margin = jnp.where((giver == sequence[0]) | (sink == sequence[0]) | (tallies[sink] == 0), 0, jnp.maximum(margin, 0))
    passed = jax.random.randint(jax.random.fold_in(own, 4), (count // 2,), 0, 1 << 20) % (margin + 1)
    tallies = tallies.at[giver].add(-passed).at[sink].add(passed)
    labels = jnp.searchsorted(jnp.cumsum(tallies), jnp.arange(rows * top), side="right").astype(jnp.int32)
    listing = labels.reshape(top, rows).T
    listing = listing[jax.random.permutation(jax.random.fold_in(own, 1), rows)]
    rotation = jax.random.randint(jax.random.fold_in(own, 2), (rows, 1), 0, top)
    return jnp.take_along_axis(listing, (jnp.arange(top)[None, :] + rotation) % top, axis=1)


def portions_of(amount, total, most, skew, full):
    weights = [(1 << 20) // math.isqrt(rank ** skew) + 1 for rank in range(1, amount + 1)]
    largest = most if full else min(most, max(-(-total // amount), total * weights[0] // sum(weights)))
    least = 1 if total - largest >= amount - 1 else 0
    given, surplus = [largest] + [least] * (amount - 1), total - largest - least * (amount - 1)
    while surplus > 0:
        movable = [i for i in range(1, amount) if given[i] < largest] or [i for i in range(1, amount) if given[i] < most]
        whole, remaining = sum([weights[i] for i in movable]), surplus
        for i in movable:
            addition = min(most - given[i], max(1, remaining * weights[i] // whole), surplus)
            given[i] = given[i] + addition
            surplus = surplus - addition
    return np.array(given)


def gaussian(own_key, dims, deviation, reach, cuts=(), kind=jnp.bfloat16):
    result = jax.random.normal(own_key, dims, jnp.float32) * deviation
    if len(cuts) > 0:
        result = steps_of(own_key, dims, cuts, -0.22, 0.18) * result
    return jnp.clip(result, min=-reach, max=reach).astype(kind)


def setup_inputs(seed: int = 0) -> dict:
    arg_keys = jax.random.split(jax.random.key(seed), 12)
    item_table = gaussian(arg_keys[0], (ITEMS, E), 1.0, 6.0, ((0, 128),))
    history_owner_keys = jax.random.split(jax.random.fold_in(arg_keys[1], 1), TOKENS // FETCH)
    history_owner_turns = jax.random.permutation(jax.random.fold_in(arg_keys[1], 3), TOKENS // FETCH)
    history_owner = jax.vmap(lambda own, number: shared_out(jax.random.fold_in(arg_keys[1], 2), own, number, FETCH, N_DP, 1, CAP, 2))(history_owner_keys, history_owner_turns).reshape((TOKENS, 1))
    history_row = with_ends(jax.random.randint(arg_keys[2], (TOKENS,), 0, ITEM_DEV), jax.random.fold_in(arg_keys[2], 1), 0, ITEM_DEV - 1).astype(jnp.int32)
    w_in = gaussian(arg_keys[3], (E, C), E ** -0.5, 0.375)
    conv_a = gaussian(arg_keys[4], (BLOCKS, 3, C, C), (3 * C) ** -0.5, 0.15625, ((3, 4),))
    conv_b = gaussian(arg_keys[5], (BLOCKS, 3, C, C), (3 * C) ** -0.5, 0.15625, ((2, 4),))
    gains = jnp.clip(1.0 + 0.1 * jax.random.normal(arg_keys[6], (BLOCKS, C), jnp.float32), 0.5, 1.5)
    w_out = gaussian(arg_keys[7], (C, E), C ** -0.5, 0.25)
    cand_row = with_ends(jax.random.randint(arg_keys[8], (USERS, N_DP, CPO), 0, ITEM_DEV), jax.random.fold_in(arg_keys[8], 1), 0, ITEM_DEV - 1).astype(jnp.int32)
    cand_count = jax.vmap(lambda own: uneven_parts(own, N_DP, NCAND, CPO, 2))(jax.random.split(arg_keys[9], USERS)).reshape((USERS, N_DP)).astype(jnp.int32)
    pos_owner = with_ends(jax.random.randint(arg_keys[10], (USERS,), 0, N_DP), jax.random.fold_in(arg_keys[10], 1), 0, N_DP - 1).astype(jnp.int32)
    return dict(item_table=item_table, history_owner=history_owner, history_row=history_row, w_in=w_in, conv_a=conv_a, conv_b=conv_b, gains=gains, w_out=w_out, cand_row=cand_row, cand_count=cand_count, pos_owner=pos_owner)


def shift_rows(values, offset):
    padded = jnp.pad(values, ((0, 0), (offset, 0), (0, 0)))
    return padded[:, :values.shape[1], :]

def causal_taps(values, dilation):
    return jnp.concatenate([values, shift_rows(values, dilation), shift_rows(values, 2 * dilation)], axis=-1)

def reference(item_table, history_owner, history_row, w_in, conv_a, conv_b, gains, w_out, cand_row, cand_count, pos_owner):
    item_ids = (history_owner[:, 0] * ITEM_DEV + history_row).astype(jnp.int32)
    embedded = item_table[item_ids]
    hidden = jnp.dot(embedded, w_in, preferred_element_type=jnp.float32).astype(jnp.bfloat16)
    hidden = hidden.reshape(USERS, LEN, C)
    quarter = C // N_MP
    for block_idx in range(BLOCKS):
        dilation = 1 if block_idx % 2 == 0 else 4
        taps_a = causal_taps(hidden, dilation).reshape(-1, 3 * C)
        rectified = jax.nn.relu(jnp.dot(taps_a, conv_a[block_idx].reshape(3 * C, C), preferred_element_type=jnp.float32)).astype(jnp.bfloat16)
        taps_b = causal_taps(rectified.reshape(USERS, LEN, C), 2 * dilation).reshape(-1, 3, C)
        branch = jnp.zeros((USERS * LEN, C), jnp.float32)
        for shard_idx in range(N_MP):
            lhs = taps_b[:, :, shard_idx * quarter:(shard_idx + 1) * quarter].reshape(-1, 3 * quarter)
            rhs = conv_b[block_idx][:, shard_idx * quarter:(shard_idx + 1) * quarter, :].reshape(3 * quarter, C)
            partial_value = jnp.dot(lhs, rhs, preferred_element_type=jnp.float32).astype(jnp.bfloat16)
            partial_value = lax.optimization_barrier(partial_value)
            branch = branch + partial_value.astype(jnp.float32)
        summed = hidden.reshape(-1, C).astype(jnp.float32) + branch
        row_mean = lax.optimization_barrier(jnp.mean(summed, axis=1, keepdims=True))
        row_msq = lax.optimization_barrier(jnp.mean(summed * summed, axis=1, keepdims=True))
        row_var = row_msq - row_mean * row_mean
        normed = (summed - row_mean) * lax.rsqrt(row_var + 1e-05) * gains[block_idx]
        hidden = normed.astype(jnp.bfloat16).reshape(USERS, LEN, C)
    last_rows = hidden[:, LEN - 1, :]
    user_vec = jnp.dot(last_rows, w_out, preferred_element_type=jnp.float32).astype(jnp.bfloat16)
    owner_base = (jnp.arange(N_DP, dtype=jnp.int32) * ITEM_DEV)[None, :, None]
    cand_rows = item_table[(owner_base + cand_row).astype(jnp.int32)]
    raw_scores = 0.25 * jnp.einsum('ue,uoce->uoc', user_vec.astype(jnp.float32), cand_rows.astype(jnp.float32))
    valid_slot = jnp.arange(CPO, dtype=jnp.int32)[None, None, :] < cand_count[:, :, None]
    scores = jnp.where(valid_slot, raw_scores, 0.0)
    exp_total = lax.optimization_barrier(jnp.sum(jnp.where(valid_slot, jnp.exp(raw_scores), 0.0), axis=(1, 2)))
    positive = jnp.take_along_axis(raw_scores[:, :, 0], pos_owner[:, None], axis=1)[:, 0]
    user_loss = jnp.log(exp_total) - positive
    return (scores, user_loss)
```

```python
import jax
import jax.numpy as jnp
from jax import lax
from jax.sharding import PartitionSpec as P

C = 512
BLOCKS = 4
LEN = 256
CAP = 4
CPO = 8
REACH = 61
WINDOW = 64
READ_FROM = (0, 32, 32, 56)

F32 = jnp.float32
BF16 = jnp.bfloat16


def exchange(values, axis):
    return lax.all_to_all(values, axis, split_axis=0, concat_axis=0, tiled=True)


def share(values, axis_size):
    return exchange(jnp.broadcast_to(values[None], (axis_size,) + values.shape), "mp")


def shifted_sum(parts, gap):
    total = parts[0]
    for k in (1, 2):
        total = total + jnp.pad(parts[k], ((k * gap, 0), (0, 0)))[: parts[k].shape[0]]
    return total


def pick_rows(table, ids):
    onehot = (ids[:, None] == jnp.arange(table.shape[0], dtype=jnp.int32)[None, :]).astype(BF16)
    return jnp.dot(onehot, table, preferred_element_type=F32).astype(BF16)


def per_device(
    item_table,
    history_owner,
    history_row,
    w_in,
    conv_a,
    conv_b,
    gains,
    w_out,
    cand_row,
    cand_count,
    pos_owner,
):
    dp_count = lax.axis_size("dp")
    mp_count = lax.axis_size("mp")
    mp_index = lax.axis_index("mp")
    last = mp_count - 1
    owner_ids = history_owner[:, 0]
    event = jnp.arange(WINDOW, dtype=jnp.int32)
    same = owner_ids[:, None] == owner_ids[None, :]
    slot = jnp.sum((same & (event[None, :] < event[:, None])).astype(jnp.int32), axis=1)
    of_owner = owner_ids[None, :] == jnp.arange(dp_count, dtype=jnp.int32)[:, None]
    slots = jnp.arange(CAP, dtype=jnp.int32)
    placed = of_owner[:, None, :] & (slot[None, :] == slots[:, None])[None]
    history_asks = jnp.sum(jnp.where(placed, history_row[None, None, :], 0), axis=2)
    cand_padded = jnp.pad(cand_row[0], ((0, 0), (0, 3 * last + CAP - CPO)))
    cand_asks = lax.dynamic_slice(
        cand_padded, (0, 3 * jnp.minimum(mp_index, last - 1)), (dp_count, CAP)
    )
    asks = jnp.where(mp_index == last, history_asks, cand_asks)
    asked = exchange(jnp.pad(asks, ((0, 0), (0, 16 - CAP))), "dp")[:, :CAP]
    picked = pick_rows(item_table, asked.reshape(-1)).reshape(dp_count, CAP, -1)
    arrived = exchange(picked, "dp")
    embedded = pick_rows(arrived.reshape(dp_count * CAP, -1), owner_ids * CAP + slot)
    embedded = share(embedded, mp_count)[last]
    hidden = jnp.dot(embedded, w_in, preferred_element_type=F32).astype(BF16)
    cand_all = share(arrived, mp_count)
    cand_rows = jnp.concatenate(
        [cand_all[0][:, :3], cand_all[1][:, :3], cand_all[2][:, : CPO - 6]], axis=1
    )
    for block_idx in range(BLOCKS):
        gap = 1 if block_idx % 2 == 0 else 4
        rectified = jax.nn.relu(
            shifted_sum(
                [jnp.dot(hidden, conv_a[block_idx, k], preferred_element_type=F32) for k in range(3)],
                gap,
            )
        ).astype(BF16)
        partial_value = shifted_sum(
            [jnp.dot(rectified, conv_b[block_idx, k], preferred_element_type=F32) for k in range(3)],
            2 * gap,
        ).astype(BF16)
        keep = READ_FROM[block_idx] - (WINDOW - hidden.shape[0])
        parts = share(partial_value[keep:], mp_count).astype(F32)
        summed = hidden[keep:].astype(F32) + (parts[0] + parts[1] + parts[2] + parts[3])
        row_mean = jnp.mean(summed, axis=1, keepdims=True)
        row_msq = jnp.mean(summed * summed, axis=1, keepdims=True)
        row_var = row_msq - row_mean * row_mean
        hidden = ((summed - row_mean) * lax.rsqrt(row_var + 1e-05) * gains[block_idx]).astype(BF16)
    user_vec = jnp.dot(hidden[-1:], w_out, preferred_element_type=F32).astype(BF16)
    raw_scores = 0.25 * jnp.einsum(
        "ue,nce->unc", user_vec, cand_rows, preferred_element_type=F32
    )
    valid_slot = jnp.arange(CPO, dtype=jnp.int32)[None, None, :] < cand_count[:, :, None]
    scores = jnp.where(valid_slot, raw_scores, 0.0)
    exp_total = jnp.sum(jnp.where(valid_slot, jnp.exp(raw_scores), 0.0), axis=(1, 2))
    is_positive = jnp.arange(dp_count, dtype=jnp.int32)[None, :] == pos_owner[:, None]
    positive = jnp.sum(jnp.where(is_positive, raw_scores[:, :, 0], 0.0), axis=1)
    user_loss = jnp.log(exp_total) - positive
    return (scores, user_loss)


def solution(mesh):
    return jax.shard_map(
        per_device,
        mesh=mesh,
        in_specs=(
            P("dp", None),
            P(("dp", "mp"), None),
            P(("dp", "mp")),
            P(),
            P(None, None, None, "mp"),
            P(None, None, "mp", None),
            P(),
            P(),
            P("dp", None, None),
            P("dp", None),
            P("dp"),
        ),
        out_specs=(P("dp", None, None), P("dp")),
        check_vma=False,
    )
```

```python
import jax
import jax.numpy as jnp
from jax import lax
from jax.experimental import pallas as pl
from jax.experimental.pallas import tpu as pltpu
from jax.sharding import PartitionSpec as P


C = 512
QUARTER = 128
CAP = 4
CPO = 8
WINDOW = 64
LATE = 32
FIRST = 3
SECOND = 1
WEIGHT_MOVES = ((2, 0), (0, 2), (1, 3))

F32 = jnp.float32
BF16 = jnp.bfloat16
VMEM = pltpu.MemorySpace.VMEM
SMEM = pltpu.MemorySpace.SMEM


def exchange(values, axis):
    return lax.all_to_all(values, axis, split_axis=0, concat_axis=0, tiled=True)


def pick_rows(table, ids):
    onehot = (ids[:, None] == jnp.arange(table.shape[0], dtype=jnp.int32)[None, :]).astype(BF16)
    return jnp.dot(onehot, table, preferred_element_type=F32).astype(BF16)


def dot(a, b):
    return jnp.dot(a, b, preferred_element_type=F32)


def moved_down(values, rows):
    at = lax.broadcasted_iota(jnp.int32, values.shape, 0)
    return jnp.where(at < rows, 0.0, pltpu.roll(values, rows, 0))


def taps(parts, gap):
    return parts[0] + moved_down(parts[1], gap) + moved_down(parts[2], 2 * gap)


def ask_kernel(place, owner, row, cand, out):
    along = jnp.broadcast_to(owner[...].astype(F32), (128, WINDOW))
    down = jnp.transpose(jnp.concatenate([along, along], axis=1))[:WINDOW, :WINDOW]
    grid = (WINDOW, WINDOW)
    earlier = lax.broadcasted_iota(jnp.int32, grid, 0) < lax.broadcasted_iota(jnp.int32, grid, 1)
    slot = jnp.sum(jnp.where((down == along[:WINDOW]) & earlier, 1.0, 0.0), axis=0, keepdims=True)
    of_owner = along == lax.broadcasted_iota(jnp.int32, along.shape, 0).astype(F32)
    rows = row[...].astype(F32)
    lane = lax.broadcasted_iota(jnp.int32, (128, 128), 1)
    history = jnp.zeros((128, 128), F32)
    for k in range(CAP):
        column = jnp.sum(jnp.where(of_owner & (slot == k), rows, 0.0), axis=1, keepdims=True)
        history = jnp.where(lane == k, column, history)
    slots = cand[...].astype(F32)
    mp_index = place[2]
    chosen = jnp.where(
        mp_index == SECOND,
        slots[:CAP],
        jnp.where(mp_index == 0, slots[CAP:], jnp.concatenate([slots[6:], slots[6:]], axis=0)),
    )
    cands = jnp.transpose(jnp.concatenate([chosen, jnp.zeros((128 - CAP, 128), F32)], axis=0))
    out[...] = jnp.where(mp_index == FIRST, history, cands).astype(jnp.int32)[:, : out.shape[1]]


def pack_kernel(place, conv_a, conv_b, *outs):
    side = pl.multiple_of(place[0] * 256, 256)
    for (to_first, _), out in zip(WEIGHT_MOVES, outs):
        start = jnp.where(place[2] == to_first, 0, 2)
        for j in range(2):
            for k in range(3):
                out[j, pl.ds(k * 256, 256), :] = conv_a[start + j, k, pl.ds(side, 256), :]
                for half in range(2):
                    rows = pl.ds(768 + half * 384 + k * 128, 128)
                    out[j, rows, :] = conv_b[start + j, k, :, pl.ds(pl.multiple_of(side + half * 128, 128), 128)]


def block(hidden, j, gap, core_even, base, gain, conv_a, conv_b, mine, theirs):
    left, right = hidden[:, :256], hidden[:, 256:]
    at_mine = jnp.where(core_even, left, right)
    at_theirs = jnp.where(core_even, right, left)
    parts = []
    for k in range(3):
        rows = pl.ds(k * 256, 256)
        own = dot(hidden, conv_a[base + j, k])
        far = dot(at_mine, jnp.concatenate([w[j, rows, :] for w in mine], axis=1))
        far = far + dot(at_theirs, jnp.concatenate([w[j, rows, :] for w in theirs], axis=1))
        parts.append(jnp.concatenate([own, far], axis=1))
    rectified = jnp.maximum(taps(parts, gap), 0.0).astype(BF16)
    own_rect, far_rect = rectified[:, :QUARTER], rectified[:, QUARTER:]

    def columns(refs, k):
        return jnp.concatenate(
            [
                jnp.concatenate(
                    [w[j, pl.ds(768 + k * 128, 128), :], w[j, pl.ds(1152 + k * 128, 128), :]], axis=1
                )
                for w in refs
            ],
            axis=0,
        )

    own = taps([dot(own_rect, conv_b[base + j, k]) for k in range(3)], 2 * gap)
    z_mine = taps([dot(far_rect, columns(mine, k)) for k in range(3)], 2 * gap)
    z_theirs = taps([dot(far_rect, columns(theirs, k)) for k in range(3)], 2 * gap)
    far = jnp.concatenate(
        [jnp.where(core_even, z_mine, z_theirs), jnp.where(core_even, z_theirs, z_mine)], axis=1
    )
    summed = hidden.astype(F32) + own + far
    row_mean = jnp.mean(summed, axis=1, keepdims=True)
    row_msq = jnp.mean(summed * summed, axis=1, keepdims=True)
    row_var = row_msq - row_mean * row_mean
    return ((summed - row_mean) * lax.rsqrt(row_var + 1e-05) * gain).astype(BF16)


def two_blocks(hidden, stage, place, gains, conv_a, conv_b, mine, theirs):
    core_even = place[0] == 0
    base = place[1]
    for j, gap in ((0, 1), (1, 4)):
        gain = gains[pl.ds(2 * stage + j, 1), :]
        hidden = block(hidden, j, gap, core_even, base, gain, conv_a, conv_b, mine, theirs)
    return hidden


def first_kernel(place, hidden, gains, conv_a, conv_b, m0, m1, m2, t0, t1, t2, out):
    last = two_blocks(hidden[...], 0, place, gains, conv_a, conv_b, (m0, m1, m2), (t0, t1, t2))
    out[...] = last[LATE:]


def second_kernel(
    place, hidden, gains, conv_a, conv_b, m0, m1, m2, t0, t1, t2, w_out, rows_a, rows_b, rows_c, count, pos, out
):
    last = two_blocks(hidden[...], 1, place, gains, conv_a, conv_b, (m0, m1, m2), (t0, t1, t2))
    vec = dot(last[LATE - 16 :], w_out[...]).astype(BF16)

    def against(rows, per):
        scored = lax.dot_general(vec, rows[...], (((1,), (1,)), ((), ())), preferred_element_type=F32)[15:16]
        shape = (CPO, scored.shape[1])
        lane = lax.broadcasted_iota(jnp.int32, shape, 1)
        return jnp.broadcast_to(0.25 * scored, shape), lane % per

    owner_of, kept = [], []
    slot = lax.broadcasted_iota(jnp.int32, (CPO, 1), 0)
    first_slot = 0
    for rows, per in ((rows_a, 4), (rows_b, 2), (rows_c, 2)):
        scored, place_in = against(rows, per)
        kept.append(jnp.where(place_in + first_slot == slot, scored, 0.0))
        grid = (scored.shape[1], 128)
        owner_of.append(
            (lax.broadcasted_iota(jnp.int32, grid, 0) // per == lax.broadcasted_iota(jnp.int32, grid, 1)).astype(F32)
        )
        first_slot += per
    raw = jnp.dot(
        jnp.concatenate(kept, axis=1),
        jnp.concatenate(owner_of, axis=0),
        precision=lax.Precision.HIGHEST,
        preferred_element_type=F32,
    )
    valid = slot < count[...]
    total = jnp.sum(jnp.where(valid, jnp.exp(raw), 0.0), axis=(0, 1), keepdims=True)
    owner = lax.broadcasted_iota(jnp.int32, (1, 128), 1)
    positive = jnp.sum(jnp.where(owner == pos[0], raw[:1], 0.0), axis=(0, 1), keepdims=True)
    out[:CPO, :] = jnp.where(valid, raw, 0.0)
    out[CPO:, :] = jnp.broadcast_to(jnp.log(total) - positive, (CPO, 128))


def call(kernel, out_shape, operands, flops):
    in_smem = {0, len(operands) - 1} if kernel is second_kernel else {0}
    return pl.pallas_call(
        kernel,
        out_shape=out_shape,
        in_specs=[pl.BlockSpec(memory_space=SMEM if i in in_smem else VMEM) for i in range(len(operands))],
        out_specs=jax.tree.map(lambda _: pl.BlockSpec(memory_space=VMEM), out_shape),
        compiler_params=pltpu.CompilerParams(vmem_limit_bytes=24 * 1024 * 1024),
        cost_estimate=pl.CostEstimate(flops=flops, bytes_accessed=8 << 20, transcendentals=0),
    )(*operands)


def forward(
    item_table,
    history_owner,
    history_row,
    w_in,
    conv_a,
    conv_b,
    gains,
    w_out,
    cand_row,
    cand_count,
    pos_owner,
):
    dp_count = lax.axis_size("dp")
    mp_count = lax.axis_size("mp")
    dp_index = lax.axis_index("dp")
    mp_index = lax.axis_index("mp")
    base = jnp.where(mp_index == SECOND, 2, 0)
    place = jnp.stack([dp_index % 2, base, mp_index]).astype(jnp.int32)
    asks = call(
        ask_kernel,
        jax.ShapeDtypeStruct((dp_count, 16), jnp.int32),
        (place, history_owner.reshape(1, WINDOW), history_row.reshape(1, WINDOW), cand_row[0].T),
        1 << 20,
    )
    asks, pack_a, pack_b = lax.optimization_barrier((asks, conv_a, conv_b))
    asked = exchange(asks, "dp")[:, :CAP]

    sent = call(
        pack_kernel, [jax.ShapeDtypeStruct((2, 1536, 128), BF16)] * 3, (place, pack_a, pack_b), 1 << 20
    )
    mine, theirs = [], []
    for (to_first, to_second), half in zip(WEIGHT_MOVES, sent):
        mine.append(lax.ppermute(half, "mp", [(to_first, FIRST), (to_second, SECOND)]))
    for half in mine:
        theirs.append(lax.ppermute(half, "dp", [(i, i ^ 1) for i in range(dp_count)]))
    picked = pick_rows(item_table, asked.reshape(-1)).reshape(dp_count, CAP, -1)
    arrived = exchange(picked, "dp")
    arrived_rows = arrived.reshape(dp_count * CAP, -1)
    owner_ids = history_owner[:, 0]
    event = jnp.arange(WINDOW, dtype=jnp.int32)
    same = owner_ids[:, None] == owner_ids[None, :]
    slot = jnp.sum((same & (event[None, :] < event[:, None])).astype(jnp.int32), axis=1)
    embedded = pick_rows(arrived_rows, owner_ids * CAP + slot)
    hidden = jnp.dot(embedded, w_in, preferred_element_type=F32).astype(BF16)
    hidden = call(
        first_kernel,
        jax.ShapeDtypeStruct((LATE, C), BF16),
        (place, hidden, gains, conv_a, conv_b, *mine, *theirs),
        2 * 2 * 64 * 6 * 512 * 512,
    )
    hidden = lax.ppermute(hidden, "mp", [(FIRST, SECOND)])
    pair = arrived[:, :2]
    rows_b = lax.ppermute(pair, "mp", [(0, SECOND)]).reshape(2 * dp_count, -1)
    rows_c = lax.ppermute(pair, "mp", [(2, SECOND)]).reshape(2 * dp_count, -1)
    packed_out = call(
        second_kernel,
        jax.ShapeDtypeStruct((2 * CPO, dp_count), F32),
        (place, hidden, gains, conv_a, conv_b, *mine, *theirs, w_out, arrived_rows, rows_b, rows_c, cand_count, pos_owner),
        2 * 2 * 32 * 6 * 512 * 512,
    )
    shared = exchange(jnp.broadcast_to(packed_out[None], (mp_count,) + packed_out.shape), "mp")[SECOND]
    return (shared[:CPO].T[None], shared[CPO, :1])


def solution(mesh):
    return jax.shard_map(
        forward,
        mesh=mesh,
        in_specs=(
            P("dp", None),
            P(("dp", "mp"), None),
            P(("dp", "mp")),
            P(),
            P(None, None, None, "mp"),
            P(None, None, "mp", None),
            P(),
            P(),
            P("dp", None, None),
            P("dp", None),
            P("dp"),
        ),
        out_specs=(P("dp", None, None), P("dp")),
        check_vma=False,
    )
```

```python
import jax
import jax.numpy as jnp
from jax import lax
from jax.experimental import pallas as pl
from jax.experimental.pallas import tpu as pltpu
from jax.sharding import PartitionSpec as P


C = 512
QUARTER = 128
BLOCKS = 4
CAP = 4
CPO = 8
WINDOW = 64
LATE = 32
FIRST = 3
SECOND = 1
WEIGHT_MOVES = ((2, 0), (0, 2), (1, 3))

F32 = jnp.float32
BF16 = jnp.bfloat16
VMEM = pltpu.MemorySpace.VMEM
SMEM = pltpu.MemorySpace.SMEM
HBM = pltpu.MemorySpace.HBM
MIB = 1024 * 1024
WEIGHTS = (2, 4, 3, 128, 128)


def exchange(values, axis):
    return lax.all_to_all(values, axis, split_axis=0, concat_axis=0, tiled=True)


def dot(a, b):
    return jnp.dot(a, b, preferred_element_type=F32)


def dot_t(a, b):
    return lax.dot_general(a, b, (((1,), (1,)), ((), ())), preferred_element_type=F32)


def iota(shape, axis):
    return lax.broadcasted_iota(jnp.int32, shape, axis)


def core_of():
    return lax.rem(lax.axis_index("dp"), 2)


def start_all(copies):
    for copy in copies:
        copy.start()


def wait_all(copies):
    for copy in copies:
        copy.wait()


def moved_down(values, rows):
    return jnp.where(iota(values.shape, 0) < rows, 0.0, pltpu.roll(values, rows, 0))


def taps(parts, gap):
    return parts[0] + moved_down(parts[1], gap) + moved_down(parts[2], 2 * gap)


def ask_kernel(owner, row, cand, out, code, owner_v, row_v, cand_v, sems):
    copies = [
        pltpu.make_async_copy(owner, owner_v, sems.at[0]),
        pltpu.make_async_copy(row, row_v, sems.at[1]),
        pltpu.make_async_copy(cand, cand_v, sems.at[2]),
    ]
    start_all(copies)
    wait_all(copies)
    along = jnp.broadcast_to(owner_v[...].astype(F32), (128, WINDOW))
    down = jnp.transpose(jnp.concatenate([along, along], axis=1))[:WINDOW, :WINDOW]
    grid = (WINDOW, WINDOW)
    same = down == along[:WINDOW]
    first, second = iota(grid, 0), iota(grid, 1)
    slot = jnp.sum(jnp.where(same & (first < second), 1.0, 0.0), axis=0, keepdims=True)
    slot_down = jnp.sum(jnp.where(same & (second < first), 1.0, 0.0), axis=1, keepdims=True)
    code[...] = jnp.broadcast_to(8.0 * down[:, :1] + slot_down, (WINDOW, 128)).astype(jnp.int32)
    of_owner = along == iota(along.shape, 0).astype(F32)
    rows = row_v[...].astype(F32)
    lane = iota((128, 128), 1)
    history = jnp.zeros((128, 128), F32)
    for k in range(CAP):
        column = jnp.sum(jnp.where(of_owner & (slot == k), rows, 0.0), axis=1, keepdims=True)
        history = jnp.where(lane == k, column, history)
    slots = cand_v[...].astype(F32)
    mp_index = lax.axis_index("mp")
    chosen = jnp.where(mp_index == SECOND, slots[:CAP], slots[CAP:])
    cands = jnp.transpose(jnp.concatenate([chosen, jnp.zeros((128 - CAP, 128), F32)], axis=0))
    out[...] = jnp.where(mp_index == FIRST, history, cands).astype(jnp.int32)[:, : out.shape[1]]


def pack_kernel(conv_a, conv_b, out_0, out_1, out_2, packed, sems):
    side = pl.multiple_of(core_of() * 256, 256)
    mp_index = lax.axis_index("mp")
    loads = []
    for half in range(2):
        at = pl.ds(pl.multiple_of(side + half * 128, 128), 128)
        loads.append(pltpu.make_async_copy(conv_a.at[:, :, at, :], packed.at[:, half], sems.at[half]))
        loads.append(pltpu.make_async_copy(conv_b.at[:, :, :, at], packed.at[:, 2 + half], sems.at[2 + half]))
    start_all(loads)
    wait_all(loads)
    stores = []
    for i, ((to_first, _), out) in enumerate(zip(WEIGHT_MOVES, (out_0, out_1, out_2))):
        start = jnp.where(mp_index == to_first, 0, 2)
        stores.append(pltpu.make_async_copy(packed.at[pl.ds(start, 2)], out, sems.at[4 + i]))
    start_all(stores)
    wait_all(stores)


def pick_kernel(asked, table, out):
    count = out.shape[0]
    spread = (iota((count, 128), 0) // 8 == iota((count, 128), 1)).astype(BF16)
    wanted = asked[...]
    high = dot(spread, (wanted // 64).astype(F32).astype(BF16))
    low = dot(spread, (wanted % 64).astype(F32).astype(BF16))
    here = iota(high.shape, 0) % 4 == iota(high.shape, 1)
    ids = jnp.sum(jnp.where(here, 64.0 * high + low, 0.0), axis=1, keepdims=True).astype(jnp.int32)
    rows = 256
    for at in range(0, count, rows):
        onehot = (ids[at : at + rows] == iota((rows, table.shape[0]), 1)).astype(F32).astype(BF16)
        both = dot(onehot, table[...])
        second = iota((rows, 128), 0) % 8 >= 4
        out[at : at + rows, :] = jnp.where(second, both[:, 128:], both[:, :128]).astype(BF16)


def block(hidden, j, gap, core_even, gain, conv_a, conv_b, mine, theirs):
    left, right = hidden[:, :256], hidden[:, 256:]
    at_mine = jnp.where(core_even, left, right)
    at_theirs = jnp.where(core_even, right, left)

    def split(ref, k):
        both = [jnp.concatenate([ref[i, j, half, k] for i in range(3)], axis=1) for half in range(2)]
        return jnp.concatenate(both, axis=0)

    parts = []
    for k in range(3):
        own = dot(hidden, conv_a[j, k])
        far = dot(at_mine, split(mine, k)) + dot(at_theirs, split(theirs, k))
        parts.append(jnp.concatenate([own, far], axis=1))
    rectified = jnp.maximum(taps(parts, gap), 0.0).astype(BF16)
    own_rect, far_rect = rectified[:, :QUARTER], rectified[:, QUARTER:]

    def columns(ref, k):
        return jnp.concatenate(
            [jnp.concatenate([ref[i, j, 2, k], ref[i, j, 3, k]], axis=1) for i in range(3)], axis=0
        )

    own = taps([dot(own_rect, conv_b[j, k]) for k in range(3)], 2 * gap)
    z_mine = taps([dot(far_rect, columns(mine, k)) for k in range(3)], 2 * gap)
    z_theirs = taps([dot(far_rect, columns(theirs, k)) for k in range(3)], 2 * gap)
    far = jnp.concatenate(
        [jnp.where(core_even, z_mine, z_theirs), jnp.where(core_even, z_theirs, z_mine)], axis=1
    )
    summed = hidden.astype(F32) + own + far
    row_mean = jnp.mean(summed, axis=1, keepdims=True)
    row_msq = jnp.mean(summed * summed, axis=1, keepdims=True)
    row_var = row_msq - row_mean * row_mean
    return ((summed - row_mean) * lax.rsqrt(row_var + 1e-05) * gain).astype(BF16)


def weight_copies(conv_a, conv_b, moved, own_a, own_b, mine, theirs, sems):
    base = jnp.where(lax.axis_index("mp") == SECOND, 2, 0)
    copies = []
    for j in range(2):
        pairs = [(conv_a.at[base + j], own_a.at[j]), (conv_b.at[base + j], own_b.at[j])]
        pairs += [(moved[i].at[j], mine.at[i, j]) for i in range(3)]
        pairs += [(moved[3 + i].at[j], theirs.at[i, j]) for i in range(3)]
        copies.append([pltpu.make_async_copy(a, b, sems.at[8 * j + n]) for n, (a, b) in enumerate(pairs)])
    return copies


WEIGHT_SCRATCH = (
    pltpu.VMEM((2, 3, C, QUARTER), BF16),
    pltpu.VMEM((2, 3, QUARTER, C), BF16),
    pltpu.VMEM((3,) + WEIGHTS, BF16),
    pltpu.VMEM((3,) + WEIGHTS, BF16),
    pltpu.SemaphoreType.DMA((16,)),
)


def two_blocks(hidden, stage, gains, copies, own_a, own_b, mine, theirs):
    core_even = core_of() == 0
    for j, gap in ((0, 1), (1, 4)):
        wait_all(copies[j])
        gain = gains[pl.ds(2 * stage + j, 1), :]
        hidden = block(hidden, j, gap, core_even, gain, own_a, own_b, mine, theirs)
    return hidden


def first_kernel(arrived, code, w_in, gains, conv_a, conv_b, m0, m1, m2, t0, t1, t2, out, own_a, own_b, mine, theirs, sems):
    copies = weight_copies(conv_a, conv_b, (m0, m1, m2, t0, t1, t2), own_a, own_b, mine, theirs, sems)
    start_all(copies[0])
    start_all(copies[1])
    at = code[:, :1]
    lanes = iota((WINDOW, arrived.shape[0]), 1)
    picked = [dot((at + 4 * half == lanes).astype(F32).astype(BF16), arrived[...]) for half in range(2)]
    embedded = jnp.concatenate(picked, axis=1).astype(BF16)
    hidden = dot(embedded, w_in[...]).astype(BF16)
    out[...] = two_blocks(hidden, 0, gains, copies, own_a, own_b, mine, theirs)[LATE:]


def second_kernel(
    pos, hidden, gains, conv_a, conv_b, m0, m1, m2, t0, t1, t2, w_out, near, far, count, out, own_a, own_b, mine, theirs, sems
):
    copies = weight_copies(conv_a, conv_b, (m0, m1, m2, t0, t1, t2), own_a, own_b, mine, theirs, sems)
    start_all(copies[0])
    start_all(copies[1])
    last = two_blocks(hidden[...], 1, gains, copies, own_a, own_b, mine, theirs)
    vec = dot(last[LATE - 16 :], w_out[...]).astype(BF16)
    grid = (CPO, near.shape[0])
    second = iota((1, near.shape[0]), 1) % 8 >= 4

    def scored(rows):
        halves = [dot_t(vec[:, at : at + 128], rows[...])[15:16] for at in (0, 128)]
        return jnp.broadcast_to(0.25 * jnp.where(second, halves[1], halves[0]), grid)

    slot, lane = iota(grid, 0), iota(grid, 1)
    kept = jnp.where(lane % 4 == slot % 4, jnp.where(slot < CAP, scored(near), scored(far)), 0.0)
    pieces, rest = [], kept
    for _ in range(3):
        piece = rest.astype(BF16)
        pieces.append(piece.astype(F32))
        rest = rest - piece.astype(F32)
    owners = (iota((grid[1], 128), 0) // 8 == iota((grid[1], 128), 1)).astype(F32).astype(BF16)
    sums = dot(jnp.concatenate(pieces, axis=0).astype(BF16), owners)
    raw = sums[:CPO] + sums[CPO : 2 * CPO] + sums[2 * CPO :]
    valid = iota(raw.shape, 0) < count[...]
    total = jnp.sum(jnp.where(valid, jnp.exp(raw), 0.0), axis=(0, 1), keepdims=True)
    positive = jnp.sum(jnp.where(iota((1, 128), 1) == pos[0], raw[:1], 0.0), axis=(0, 1), keepdims=True)
    out[:CPO, :] = jnp.where(valid, raw, 0.0)
    out[CPO:, :] = jnp.broadcast_to(jnp.log(total) - positive, (CPO, 128))


def call(kernel, out_shape, operands, spaces, out_space, scratch, limit):
    return pl.pallas_call(
        kernel,
        out_shape=out_shape,
        in_specs=[pl.BlockSpec(memory_space=space) for space in spaces],
        out_specs=jax.tree.map(lambda _: pl.BlockSpec(memory_space=out_space), out_shape),
        scratch_shapes=scratch,
        compiler_params=pltpu.CompilerParams(vmem_limit_bytes=limit * MIB),
        cost_estimate=pl.CostEstimate(flops=1 << 28, bytes_accessed=8 << 20, transcendentals=0),
    )(*operands)


def forward(
    item_table,
    history_owner,
    history_row,
    w_in,
    conv_a,
    conv_b,
    gains,
    w_out,
    cand_row,
    cand_count,
    pos_owner,
):
    dp_count = lax.axis_size("dp")
    mp_count = lax.axis_size("mp")
    asks, code = call(
        ask_kernel,
        [jax.ShapeDtypeStruct((dp_count, 16), jnp.int32), jax.ShapeDtypeStruct((WINDOW, 128), jnp.int32)],
        (history_owner.reshape(1, WINDOW), history_row.reshape(1, WINDOW), cand_row[0].T),
        (HBM, HBM, HBM),
        VMEM,
        [
            pltpu.VMEM((1, WINDOW), jnp.int32),
            pltpu.VMEM((1, WINDOW), jnp.int32),
            pltpu.VMEM((CPO, 128), jnp.int32),
            pltpu.SemaphoreType.DMA((3,)),
        ],
        60,
    )
    asks, pack_a, pack_b = lax.optimization_barrier((asks, conv_a, conv_b))
    asked = exchange(asks, "dp")

    sent = call(
        pack_kernel,
        [jax.ShapeDtypeStruct(WEIGHTS, BF16)] * 3,
        (pack_a, pack_b),
        (HBM, HBM),
        HBM,
        [pltpu.VMEM((BLOCKS, 4, 3, 128, 128), BF16), pltpu.SemaphoreType.DMA((7,))],
        60,
    )
    moved = []
    for (to_first, to_second), half in zip(WEIGHT_MOVES, sent):
        moved.append(lax.ppermute(half, "mp", [(to_first, FIRST), (to_second, SECOND)]))
    for half in moved[:3]:
        moved.append(lax.ppermute(half, "dp", [(i, i ^ 1) for i in range(dp_count)]))

    picked = call(
        pick_kernel,
        jax.ShapeDtypeStruct((dp_count * 8, 128), BF16),
        (asked, item_table),
        (VMEM, VMEM),
        VMEM,
        [],
        60,
    )
    arrived = exchange(picked, "dp")
    far = lax.ppermute(arrived, "mp", [(0, SECOND)])
    hidden = call(
        first_kernel,
        jax.ShapeDtypeStruct((LATE, C), BF16),
        (arrived, code, w_in, gains, conv_a, conv_b, *moved),
        (VMEM,) * 4 + (HBM,) * 8,
        VMEM,
        WEIGHT_SCRATCH,
        24,
    )
    hidden = lax.ppermute(hidden, "mp", [(FIRST, SECOND)])
    packed_out = call(
        second_kernel,
        jax.ShapeDtypeStruct((2 * CPO, dp_count), F32),
        (pos_owner, hidden, gains, conv_a, conv_b, *moved, w_out, arrived, far, cand_count),
        (SMEM, VMEM, VMEM) + (HBM,) * 8 + (VMEM,) * 4,
        VMEM,
        WEIGHT_SCRATCH,
        24,
    )
    shared = exchange(jnp.broadcast_to(packed_out[None], (mp_count,) + packed_out.shape), "mp")[SECOND]
    return (shared[:CPO].T[None], shared[CPO, :1])


def solution(mesh):
    return jax.shard_map(
        forward,
        mesh=mesh,
        in_specs=(
            P("dp", None),
            P(("dp", "mp"), None),
            P(("dp", "mp")),
            P(),
            P(None, None, None, "mp"),
            P(None, None, "mp", None),
            P(),
            P(),
            P("dp", None, None),
            P("dp", None),
            P("dp"),
        ),
        out_specs=(P("dp", None, None), P("dp")),
        check_vma=False,
    )
```

```python
import jax
import jax.numpy as jnp
from jax import lax
from jax.experimental import pallas as pl
from jax.experimental.pallas import tpu as pltpu
from jax.sharding import PartitionSpec as P


C = 512
QUARTER = 128
BLOCKS = 4
CAP = 4
CPO = 8
WINDOW = 64
LATE = 32
FIRST = 3
SECOND = 1
WEIGHT_MOVES = ((2, 0), (0, 2), (1, 3))

F32 = jnp.float32
BF16 = jnp.bfloat16
VMEM = pltpu.MemorySpace.VMEM
SMEM = pltpu.MemorySpace.SMEM
HBM = pltpu.MemorySpace.HBM
MIB = 1024 * 1024
WEIGHTS = (2, 4, 3, 128, 128)


def exchange(values, axis):
    return lax.all_to_all(values, axis, split_axis=0, concat_axis=0, tiled=True)


def dot(a, b):
    return jnp.dot(a, b, preferred_element_type=F32)


def dot_t(a, b):
    return lax.dot_general(a, b, (((1,), (1,)), ((), ())), preferred_element_type=F32)


def iota(shape, axis):
    return lax.broadcasted_iota(jnp.int32, shape, axis)


def core_of():
    return lax.rem(lax.axis_index("dp"), 2)


def start_all(copies):
    for copy in copies:
        copy.start()


def wait_all(copies):
    for copy in copies:
        copy.wait()


def moved_down(values, rows):
    return jnp.where(iota(values.shape, 0) < rows, 0.0, pltpu.roll(values, rows, 0))


def taps(parts, gap):
    return parts[0] + moved_down(parts[1], gap) + moved_down(parts[2], 2 * gap)


def ask_kernel(owner, row, cand, out, code, owner_v, row_v, cand_v, sems):
    copies = [
        pltpu.make_async_copy(owner, owner_v, sems.at[0]),
        pltpu.make_async_copy(row, row_v, sems.at[1]),
        pltpu.make_async_copy(cand, cand_v, sems.at[2]),
    ]
    start_all(copies)
    wait_all(copies)
    along = jnp.broadcast_to(owner_v[...].astype(F32), (128, WINDOW))
    down = jnp.transpose(jnp.concatenate([along, along], axis=1))[:WINDOW, :WINDOW]
    grid = (WINDOW, WINDOW)
    same = down == along[:WINDOW]
    first, second = iota(grid, 0), iota(grid, 1)
    slot = jnp.sum(jnp.where(same & (first < second), 1.0, 0.0), axis=0, keepdims=True)
    slot_down = jnp.sum(jnp.where(same & (second < first), 1.0, 0.0), axis=1, keepdims=True)
    code[...] = jnp.broadcast_to(CAP * down[:, :1] + slot_down, (WINDOW, 128)).astype(jnp.int32)
    of_owner = along == iota(along.shape, 0).astype(F32)
    rows = row_v[...].astype(F32)
    lane = iota((128, 128), 1)
    history = jnp.zeros((128, 128), F32)
    for k in range(CAP):
        column = jnp.sum(jnp.where(of_owner & (slot == k), rows, 0.0), axis=1, keepdims=True)
        history = jnp.where(lane == k, column, history)
    slots = cand_v[...].astype(F32)
    mp_index = lax.axis_index("mp")
    chosen = jnp.where(mp_index == SECOND, slots[:CAP], slots[CAP:])
    cands = jnp.transpose(jnp.concatenate([chosen, jnp.zeros((128 - CAP, 128), F32)], axis=0))
    out[...] = jnp.where(mp_index == FIRST, history, cands).astype(jnp.int32)[:, : out.shape[1]]


def pack_kernel(conv_a, conv_b, out_0, out_1, out_2, packed, sems):
    side = pl.multiple_of(core_of() * 256, 256)
    mp_index = lax.axis_index("mp")
    loads = []
    for half in range(2):
        at = pl.ds(pl.multiple_of(side + half * 128, 128), 128)
        loads.append(pltpu.make_async_copy(conv_a.at[:, :, at, :], packed.at[:, half], sems.at[half]))
        loads.append(pltpu.make_async_copy(conv_b.at[:, :, :, at], packed.at[:, 2 + half], sems.at[2 + half]))
    start_all(loads)
    wait_all(loads)
    stores = []
    for i, ((to_first, _), out) in enumerate(zip(WEIGHT_MOVES, (out_0, out_1, out_2))):
        start = jnp.where(mp_index == to_first, 0, 2)
        stores.append(pltpu.make_async_copy(packed.at[pl.ds(start, 2)], out, sems.at[4 + i]))
    start_all(stores)
    wait_all(stores)


def pick_rows(table, ids):
    onehot = (ids[:, None] == jnp.arange(table.shape[0], dtype=jnp.int32)[None, :]).astype(BF16)
    return dot(onehot, table).astype(BF16)


def block(hidden, j, gap, core_even, gain, conv_a, conv_b, mine, theirs):
    left, right = hidden[:, :256], hidden[:, 256:]
    at_mine = jnp.where(core_even, left, right)
    at_theirs = jnp.where(core_even, right, left)

    def split(ref, k):
        both = [jnp.concatenate([ref[i, j, half, k] for i in range(3)], axis=1) for half in range(2)]
        return jnp.concatenate(both, axis=0)

    parts = []
    for k in range(3):
        own = dot(hidden, conv_a[j, k])
        far = dot(at_mine, split(mine, k)) + dot(at_theirs, split(theirs, k))
        parts.append(jnp.concatenate([own, far], axis=1))
    rectified = jnp.maximum(taps(parts, gap), 0.0).astype(BF16)
    own_rect, far_rect = rectified[:, :QUARTER], rectified[:, QUARTER:]

    def columns(ref, k):
        return jnp.concatenate(
            [jnp.concatenate([ref[i, j, 2, k], ref[i, j, 3, k]], axis=1) for i in range(3)], axis=0
        )

    own = taps([dot(own_rect, conv_b[j, k]) for k in range(3)], 2 * gap)
    z_mine = taps([dot(far_rect, columns(mine, k)) for k in range(3)], 2 * gap)
    z_theirs = taps([dot(far_rect, columns(theirs, k)) for k in range(3)], 2 * gap)
    far = jnp.concatenate(
        [jnp.where(core_even, z_mine, z_theirs), jnp.where(core_even, z_theirs, z_mine)], axis=1
    )
    summed = hidden.astype(F32) + own + far
    row_mean = jnp.mean(summed, axis=1, keepdims=True)
    row_msq = jnp.mean(summed * summed, axis=1, keepdims=True)
    row_var = row_msq - row_mean * row_mean
    return ((summed - row_mean) * lax.rsqrt(row_var + 1e-05) * gain).astype(BF16)


def weight_copies(moved, mine, theirs, sems):
    copies = []
    for j in range(2):
        pairs = [(moved[i].at[j], mine.at[i, j]) for i in range(3)]
        pairs += [(moved[3 + i].at[j], theirs.at[i, j]) for i in range(3)]
        copies.append([pltpu.make_async_copy(a, b, sems.at[6 * j + n]) for n, (a, b) in enumerate(pairs)])
    return copies


KEPT = (
    jax.ShapeDtypeStruct((3,) + WEIGHTS, BF16),
    jax.ShapeDtypeStruct((3,) + WEIGHTS, BF16),
)


def two_blocks(hidden, stage, gains, own_a, own_b, mine, theirs, ready):
    core_even = core_of() == 0
    for j, gap in ((0, 1), (1, 4)):
        ready(j)
        gain = gains[pl.ds(2 * stage + j, 1), :]
        hidden = block(hidden, j, gap, core_even, gain, own_a, own_b, mine, theirs)
    return hidden


def first_kernel(arrived, code, w_in, gains, own_a, own_b, m0, m1, m2, t0, t1, t2, out, mine, theirs, sems):
    copies = weight_copies((m0, m1, m2, t0, t1, t2), mine, theirs, sems)
    start_all(copies[0])
    start_all(copies[1])
    is_first = lax.axis_index("mp") == FIRST

    @pl.when(is_first)
    def _():
        onehot = (code[:, :1] == iota((WINDOW, arrived.shape[0]), 1)).astype(F32).astype(BF16)
        hidden = dot(dot(onehot, arrived[...]).astype(BF16), w_in[...]).astype(BF16)
        ready = lambda j: wait_all(copies[j])
        out[...] = two_blocks(hidden, 0, gains, own_a, own_b, mine, theirs, ready)[LATE:]

    @pl.when(jnp.logical_not(is_first))
    def _():
        wait_all(copies[0])
        wait_all(copies[1])


def second_kernel(pos, hidden, gains, own_a, own_b, mine, theirs, w_out, near, far, count, out):
    @pl.when(lax.axis_index("mp") == SECOND)
    def _():
        last = two_blocks(hidden[...], 1, gains, own_a, own_b, mine, theirs, lambda j: None)
        score(dot(last[LATE - 16 :], w_out[...]).astype(BF16), pos, near, far, count, out)


def score(vec, pos, near, far, count, out):
    grid = (CPO, near.shape[0])

    def scored(rows):
        return jnp.broadcast_to(0.25 * dot_t(vec, rows[...])[15:16], grid)

    slot, lane = iota(grid, 0), iota(grid, 1)
    kept = jnp.where(lane % CAP == slot % CAP, jnp.where(slot < CAP, scored(near), scored(far)), 0.0)
    pieces, rest = [], kept
    for _ in range(3):
        piece = rest.astype(BF16)
        pieces.append(piece.astype(F32))
        rest = rest - piece.astype(F32)
    owners = (iota((grid[1], 128), 0) // CAP == iota((grid[1], 128), 1)).astype(F32).astype(BF16)
    sums = dot(jnp.concatenate(pieces, axis=0).astype(BF16), owners)
    raw = sums[:CPO] + sums[CPO : 2 * CPO] + sums[2 * CPO :]
    valid = iota(raw.shape, 0) < count[...]
    total = jnp.sum(jnp.where(valid, jnp.exp(raw), 0.0), axis=(0, 1), keepdims=True)
    positive = jnp.sum(jnp.where(iota((1, 128), 1) == pos[0], raw[:1], 0.0), axis=(0, 1), keepdims=True)
    out[:CPO, :] = jnp.where(valid, raw, 0.0)
    out[CPO:, :] = jnp.broadcast_to(jnp.log(total) - positive, (CPO, 128))


def call(kernel, out_shape, operands, spaces, out_space, scratch, limit):
    return pl.pallas_call(
        kernel,
        out_shape=out_shape,
        in_specs=[pl.BlockSpec(memory_space=space) for space in spaces],
        out_specs=jax.tree.map(lambda _: pl.BlockSpec(memory_space=out_space), out_shape),
        scratch_shapes=scratch,
        compiler_params=pltpu.CompilerParams(vmem_limit_bytes=limit * MIB),
        cost_estimate=pl.CostEstimate(flops=1 << 28, bytes_accessed=8 << 20, transcendentals=0),
    )(*operands)


def forward(
    item_table,
    history_owner,
    history_row,
    w_in,
    conv_a,
    conv_b,
    gains,
    w_out,
    cand_row,
    cand_count,
    pos_owner,
):
    dp_count = lax.axis_size("dp")
    mp_count = lax.axis_size("mp")
    asks, code = call(
        ask_kernel,
        [jax.ShapeDtypeStruct((dp_count, 16), jnp.int32), jax.ShapeDtypeStruct((WINDOW, 128), jnp.int32)],
        (history_owner.reshape(1, WINDOW), history_row.reshape(1, WINDOW), cand_row[0].T),
        (HBM, HBM, HBM),
        VMEM,
        [
            pltpu.VMEM((1, WINDOW), jnp.int32),
            pltpu.VMEM((1, WINDOW), jnp.int32),
            pltpu.VMEM((CPO, 128), jnp.int32),
            pltpu.SemaphoreType.DMA((3,)),
        ],
        60,
    )
    asks, pack_a, pack_b = lax.optimization_barrier((asks, conv_a, conv_b))
    asked = exchange(asks, "dp")

    sent = call(
        pack_kernel,
        [jax.ShapeDtypeStruct(WEIGHTS, BF16)] * 3,
        (pack_a, pack_b),
        (HBM, HBM),
        HBM,
        [pltpu.VMEM((BLOCKS, 4, 3, 128, 128), BF16), pltpu.SemaphoreType.DMA((7,))],
        60,
    )
    moved = []
    for (to_first, to_second), half in zip(WEIGHT_MOVES, sent):
        moved.append(lax.ppermute(half, "mp", [(to_first, FIRST), (to_second, SECOND)]))
    for half in moved[:3]:
        moved.append(lax.ppermute(half, "dp", [(i, i ^ 1) for i in range(dp_count)]))

    picked = pick_rows(item_table, asked[:, :CAP].reshape(-1)).reshape(dp_count, CAP, -1)
    arrived = exchange(picked, "dp").reshape(dp_count * CAP, -1)
    base = jnp.where(lax.axis_index("mp") == SECOND, 2, 0)
    own_a = lax.dynamic_slice_in_dim(pack_a, base, 2)
    own_b = lax.dynamic_slice_in_dim(pack_b, base, 2)
    far = lax.ppermute(arrived, "mp", [(0, SECOND)])
    hidden, *kept = call(
        first_kernel,
        (jax.ShapeDtypeStruct((LATE, C), BF16),) + KEPT,
        (arrived, code, w_in, gains, own_a, own_b, *moved),
        (VMEM,) * 6 + (HBM,) * 6,
        VMEM,
        [pltpu.SemaphoreType.DMA((12,))],
        16,
    )
    hidden = lax.ppermute(hidden, "mp", [(FIRST, SECOND)])
    packed_out = call(
        second_kernel,
        jax.ShapeDtypeStruct((2 * CPO, dp_count), F32),
        (pos_owner, hidden, gains, own_a, own_b, *kept, w_out, arrived, far, cand_count),
        (SMEM,) + (VMEM,) * 10,
        VMEM,
        [],
        8,
    )
    shared = exchange(jnp.broadcast_to(packed_out[None], (mp_count,) + packed_out.shape), "mp")[SECOND]
    return (shared[:CPO].T[None], shared[CPO, :1])


def solution(mesh):
    return jax.shard_map(
        forward,
        mesh=mesh,
        in_specs=(
            P("dp", None),
            P(("dp", "mp"), None),
            P(("dp", "mp")),
            P(),
            P(None, None, None, "mp"),
            P(None, None, "mp", None),
            P(),
            P(),
            P("dp", None, None),
            P("dp", None),
            P("dp"),
        ),
        out_specs=(P("dp", None, None), P("dp")),
        check_vma=False,
    )
```

```python
import jax
import jax.numpy as jnp
from jax import lax
from jax.experimental import pallas as pl
from jax.experimental.pallas import tpu as pltpu
from jax.sharding import PartitionSpec as P


C = 512
QUARTER = 128
BLOCKS = 4
CAP = 4
CPO = 8
WINDOW = 64
LATE = 32
FIRST = 3
SECOND = 1
WEIGHT_MOVES = ((2, 0), (0, 2), (1, 3))

F32 = jnp.float32
BF16 = jnp.bfloat16
VMEM = pltpu.MemorySpace.VMEM
SMEM = pltpu.MemorySpace.SMEM
HBM = pltpu.MemorySpace.HBM
MIB = 1024 * 1024
WEIGHTS = (2, 4, 3, 128, 128)


def exchange(values, axis):
    return lax.all_to_all(values, axis, split_axis=0, concat_axis=0, tiled=True)


def dot(a, b):
    return jnp.dot(a, b, preferred_element_type=F32)


def dot_t(a, b):
    return lax.dot_general(a, b, (((1,), (1,)), ((), ())), preferred_element_type=F32)


def iota(shape, axis):
    return lax.broadcasted_iota(jnp.int32, shape, axis)


def core_of():
    return lax.rem(lax.axis_index("dp"), 2)


def start_all(copies):
    for copy in copies:
        copy.start()


def wait_all(copies):
    for copy in copies:
        copy.wait()


def moved_down(values, rows):
    return jnp.where(iota(values.shape, 0) < rows, 0.0, pltpu.roll(values, rows, 0))


def taps(parts, gap):
    return parts[0] + moved_down(parts[1], gap) + moved_down(parts[2], 2 * gap)


def ask_kernel(owner, row, cand, out, code, owner_v, row_v, cand_v, sems):
    copies = [
        pltpu.make_async_copy(owner, owner_v, sems.at[0]),
        pltpu.make_async_copy(row, row_v, sems.at[1]),
        pltpu.make_async_copy(cand, cand_v, sems.at[2]),
    ]
    start_all(copies)
    wait_all(copies)
    along = jnp.broadcast_to(owner_v[...].astype(F32), (128, WINDOW))
    down = jnp.transpose(jnp.concatenate([along, along], axis=1))[:WINDOW, :WINDOW]
    grid = (WINDOW, WINDOW)
    same = down == along[:WINDOW]
    first, second = iota(grid, 0), iota(grid, 1)
    slot = jnp.sum(jnp.where(same & (first < second), 1.0, 0.0), axis=0, keepdims=True)
    slot_down = jnp.sum(jnp.where(same & (second < first), 1.0, 0.0), axis=1, keepdims=True)
    code[...] = jnp.broadcast_to(CAP * down[:, :1] + slot_down, (WINDOW, 128)).astype(jnp.int32)
    of_owner = along == iota(along.shape, 0).astype(F32)
    rows = row_v[...].astype(F32)
    lane = iota((128, 128), 1)
    history = jnp.zeros((128, 128), F32)
    for k in range(CAP):
        column = jnp.sum(jnp.where(of_owner & (slot == k), rows, 0.0), axis=1, keepdims=True)
        history = jnp.where(lane == k, column, history)
    slots = cand_v[...].astype(F32)
    mp_index = lax.axis_index("mp")
    chosen = jnp.where(mp_index == SECOND, slots[:CAP], slots[CAP:])
    cands = jnp.transpose(jnp.concatenate([chosen, jnp.zeros((128 - CAP, 128), F32)], axis=0))
    out[...] = jnp.where(mp_index == FIRST, history, cands).astype(jnp.int32)[:, : out.shape[1]]


def pack_kernel(conv_a, conv_b, out_0, out_1, out_2, out_3, packed, sems):
    side = pl.multiple_of(core_of() * 256, 256)
    mp_index = lax.axis_index("mp")
    loads = []
    for half in range(2):
        at = pl.ds(pl.multiple_of(side + half * 128, 128), 128)
        loads.append(pltpu.make_async_copy(conv_a.at[:, :, at, :], packed.at[:, half], sems.at[half]))
        loads.append(pltpu.make_async_copy(conv_b.at[:, :, :, at], packed.at[:, 2 + half], sems.at[2 + half]))
    start_all(loads)
    wait_all(loads)
    stores = []
    outs = ((out_0, 0, 0, 2), (out_1, 1, 0, 2), (out_2, 2, 0, 1), (out_3, 2, 1, 1))
    for i, (out, move, skip, blocks) in enumerate(outs):
        start = jnp.where(mp_index == WEIGHT_MOVES[move][0], 0, 2) + skip
        stores.append(pltpu.make_async_copy(packed.at[pl.ds(start, blocks)], out, sems.at[4 + i]))
    start_all(stores)
    wait_all(stores)


def pick_rows(table, ids):
    onehot = (ids[:, None] == jnp.arange(table.shape[0], dtype=jnp.int32)[None, :]).astype(BF16)
    return dot(onehot, table).astype(BF16)


def block(hidden, j, gap, core_even, gain, conv_a, conv_b, mine, theirs):
    left, right = hidden[:, :256], hidden[:, 256:]
    at_mine = jnp.where(core_even, left, right)
    at_theirs = jnp.where(core_even, right, left)

    def split(ref, k):
        both = [jnp.concatenate([ref[i, j, half, k] for i in range(3)], axis=1) for half in range(2)]
        return jnp.concatenate(both, axis=0)

    parts = []
    for k in range(3):
        own = dot(hidden, conv_a[j, k])
        far = dot(at_mine, split(mine, k)) + dot(at_theirs, split(theirs, k))
        parts.append(jnp.concatenate([own, far], axis=1))
    rectified = jnp.maximum(taps(parts, gap), 0.0).astype(BF16)
    own_rect, far_rect = rectified[:, :QUARTER], rectified[:, QUARTER:]

    def columns(ref, k):
        return jnp.concatenate(
            [jnp.concatenate([ref[i, j, 2, k], ref[i, j, 3, k]], axis=1) for i in range(3)], axis=0
        )

    own = taps([dot(own_rect, conv_b[j, k]) for k in range(3)], 2 * gap)
    z_mine = taps([dot(far_rect, columns(mine, k)) for k in range(3)], 2 * gap)
    z_theirs = taps([dot(far_rect, columns(theirs, k)) for k in range(3)], 2 * gap)
    far = jnp.concatenate(
        [jnp.where(core_even, z_mine, z_theirs), jnp.where(core_even, z_theirs, z_mine)], axis=1
    )
    summed = hidden.astype(F32) + own + far
    row_mean = jnp.mean(summed, axis=1, keepdims=True)
    row_msq = jnp.mean(summed * summed, axis=1, keepdims=True)
    row_var = row_msq - row_mean * row_mean
    return ((summed - row_mean) * lax.rsqrt(row_var + 1e-05) * gain).astype(BF16)


def weight_copies(moved, mine, theirs, sems):
    copies = []
    for j in range(2):
        pairs = []
        for into, (whole_0, whole_1, *blocks) in ((mine, moved[:4]), (theirs, moved[4:])):
            pairs += [(whole_0.at[j], into.at[0, j]), (whole_1.at[j], into.at[1, j]), (blocks[j].at[0], into.at[2, j])]
        copies.append([pltpu.make_async_copy(a, b, sems.at[6 * j + n]) for n, (a, b) in enumerate(pairs)])
    return copies


KEPT = (
    jax.ShapeDtypeStruct((3,) + WEIGHTS, BF16),
    jax.ShapeDtypeStruct((3,) + WEIGHTS, BF16),
)


def two_blocks(hidden, stage, gains, own_a, own_b, mine, theirs, ready):
    core_even = core_of() == 0
    for j, gap in ((0, 1), (1, 4)):
        ready(j)
        gain = gains[pl.ds(2 * stage + j, 1), :]
        hidden = block(hidden, j, gap, core_even, gain, own_a, own_b, mine, theirs)
    return hidden


def first_kernel(arrived, code, w_in, gains, own_a, own_b, *refs):
    *moved, out, mine, theirs, sems = refs
    copies = weight_copies(moved, mine, theirs, sems)
    start_all(copies[0])
    start_all(copies[1])
    is_first = lax.axis_index("mp") == FIRST

    @pl.when(is_first)
    def _():
        onehot = (code[:, :1] == iota((WINDOW, arrived.shape[0]), 1)).astype(F32).astype(BF16)
        hidden = dot(dot(onehot, arrived[...]).astype(BF16), w_in[...]).astype(BF16)
        ready = lambda j: wait_all(copies[j])
        out[...] = two_blocks(hidden, 0, gains, own_a, own_b, mine, theirs, ready)[LATE:]

    @pl.when(jnp.logical_not(is_first))
    def _():
        wait_all(copies[0])
        wait_all(copies[1])


def second_kernel(pos, hidden, gains, own_a, own_b, mine, theirs, w_out, near, far, count, out):
    @pl.when(lax.axis_index("mp") == SECOND)
    def _():
        last = two_blocks(hidden[...], 1, gains, own_a, own_b, mine, theirs, lambda j: None)
        score(dot(last[LATE - 16 :], w_out[...]).astype(BF16), pos, near, far, count, out)


def score(vec, pos, near, far, count, out):
    grid = (CPO, near.shape[0])

    def scored(rows):
        return jnp.broadcast_to(0.25 * dot_t(vec, rows[...])[15:16], grid)

    slot, lane = iota(grid, 0), iota(grid, 1)
    kept = jnp.where(lane % CAP == slot % CAP, jnp.where(slot < CAP, scored(near), scored(far)), 0.0)
    pieces, rest = [], kept
    for _ in range(3):
        piece = rest.astype(BF16)
        pieces.append(piece.astype(F32))
        rest = rest - piece.astype(F32)
    owners = (iota((grid[1], 128), 0) // CAP == iota((grid[1], 128), 1)).astype(F32).astype(BF16)
    sums = dot(jnp.concatenate(pieces, axis=0).astype(BF16), owners)
    raw = sums[:CPO] + sums[CPO : 2 * CPO] + sums[2 * CPO :]
    valid = iota(raw.shape, 0) < count[...]
    total = jnp.sum(jnp.where(valid, jnp.exp(raw), 0.0), axis=(0, 1), keepdims=True)
    positive = jnp.sum(jnp.where(iota((1, 128), 1) == pos[0], raw[:1], 0.0), axis=(0, 1), keepdims=True)
    out[:CPO, :] = jnp.where(valid, raw, 0.0)
    out[CPO:, :] = jnp.broadcast_to(jnp.log(total) - positive, (CPO, 128))


def call(kernel, out_shape, operands, spaces, out_space, scratch, limit):
    return pl.pallas_call(
        kernel,
        out_shape=out_shape,
        in_specs=[pl.BlockSpec(memory_space=space) for space in spaces],
        out_specs=jax.tree.map(lambda _: pl.BlockSpec(memory_space=out_space), out_shape),
        scratch_shapes=scratch,
        compiler_params=pltpu.CompilerParams(vmem_limit_bytes=limit * MIB),
        cost_estimate=pl.CostEstimate(flops=1 << 28, bytes_accessed=8 << 20, transcendentals=0),
    )(*operands)


def forward(
    item_table,
    history_owner,
    history_row,
    w_in,
    conv_a,
    conv_b,
    gains,
    w_out,
    cand_row,
    cand_count,
    pos_owner,
):
    dp_count = lax.axis_size("dp")
    mp_count = lax.axis_size("mp")
    asks, code = call(
        ask_kernel,
        [jax.ShapeDtypeStruct((dp_count, 16), jnp.int32), jax.ShapeDtypeStruct((WINDOW, 128), jnp.int32)],
        (history_owner.reshape(1, WINDOW), history_row.reshape(1, WINDOW), cand_row[0].T),
        (HBM, HBM, HBM),
        VMEM,
        [
            pltpu.VMEM((1, WINDOW), jnp.int32),
            pltpu.VMEM((1, WINDOW), jnp.int32),
            pltpu.VMEM((CPO, 128), jnp.int32),
            pltpu.SemaphoreType.DMA((3,)),
        ],
        60,
    )
    asks, pack_a, pack_b = lax.optimization_barrier((asks, conv_a, conv_b))
    asked = exchange(asks, "dp")

    sent = call(
        pack_kernel,
        [jax.ShapeDtypeStruct(WEIGHTS, BF16)] * 2 + [jax.ShapeDtypeStruct((1,) + WEIGHTS[1:], BF16)] * 2,
        (pack_a, pack_b),
        (HBM, HBM),
        HBM,
        [pltpu.VMEM((BLOCKS, 4, 3, 128, 128), BF16), pltpu.SemaphoreType.DMA((8,))],
        60,
    )
    moved = []
    for (to_first, to_second), half in zip(WEIGHT_MOVES, sent):
        moved.append(lax.ppermute(half, "mp", [(to_first, FIRST), (to_second, SECOND)]))
    halfway = lax.ppermute(sent[3], "mp", [(1, 2), (3, 0)])
    moved.append(lax.ppermute(halfway, "mp", [(2, FIRST), (0, SECOND)]))
    base = jnp.where(lax.axis_index("mp") == SECOND, 2, 0)
    own_a = lax.dynamic_slice_in_dim(pack_a, base, 2)
    own_b = lax.dynamic_slice_in_dim(pack_b, base, 2)
    first_swap, own_a, own_b = lax.optimization_barrier((moved[0], own_a, own_b))
    for half in [first_swap] + moved[1:]:
        moved.append(lax.ppermute(half, "dp", [(i, i ^ 1) for i in range(dp_count)]))

    picked = pick_rows(item_table, asked[:, :CAP].reshape(-1)).reshape(dp_count, CAP, -1)
    arrived = exchange(picked, "dp").reshape(dp_count * CAP, -1)
    far = lax.ppermute(arrived, "mp", [(0, SECOND)])
    hidden, *kept = call(
        first_kernel,
        (jax.ShapeDtypeStruct((LATE, C), BF16),) + KEPT,
        (arrived, code, w_in, gains, own_a, own_b, *moved),
        (VMEM,) * 6 + (HBM,) * 8,
        VMEM,
        [pltpu.SemaphoreType.DMA((12,))],
        16,
    )
    hidden = lax.ppermute(hidden, "mp", [(FIRST, SECOND)])
    packed_out = call(
        second_kernel,
        jax.ShapeDtypeStruct((2 * CPO, dp_count), F32),
        (pos_owner, hidden, gains, own_a, own_b, *kept, w_out, arrived, far, cand_count),
        (SMEM,) + (VMEM,) * 10,
        VMEM,
        [],
        8,
    )
    shared = exchange(jnp.broadcast_to(packed_out[None], (mp_count,) + packed_out.shape), "mp")[SECOND]
    return (shared[:CPO].T[None], shared[CPO, :1])


def solution(mesh):
    return jax.shard_map(
        forward,
        mesh=mesh,
        in_specs=(
            P("dp", None),
            P(("dp", "mp"), None),
            P(("dp", "mp")),
            P(),
            P(None, None, None, "mp"),
            P(None, None, "mp", None),
            P(),
            P(),
            P("dp", None, None),
            P("dp", None),
            P("dp"),
        ),
        out_specs=(P("dp", None, None), P("dp")),
        check_vma=False,
    )
```
